32 devices in a mesh: dp: 2 (over x), seq: 16 (over z, y, core).
Axes of the slice: x: 2, y: 2, z: 4, core: 2. Of those that a mesh axis runs over, the one named last changes fastest.
Arguments:
- queries: bfloat16 [4096, 1024], P(('dp', 'seq')), parts along dimension 0, may hold values from -6 to 6
- keys: bfloat16 [4096, 1024], P(('dp', 'seq')), parts along dimension 0, may hold values from -6 to 6
- values: bfloat16 [4096, 1024], P(('dp', 'seq')), parts along dimension 0, may hold values from -36 to 36
- feat_weight: bfloat16 [16, 64, 256], replicated, may hold values from -0.75 to 0.75
- norm_gain: bfloat16 [1024], replicated, may hold values from 0.25 to 1.75
- counts: int32 [32, 16], P('dp'), parts along dimension 0, may hold values from 4 to 12, as said below
- offsets: int32 [32, 16], P('dp'), parts along dimension 0, may hold values from 0 to 127, as said below
Outputs:
- mixed: bfloat16 [4096, 1024], P(('dp', 'seq')), parts along dimension 0
The draws below stay inside these ranges and needn't reach their ends.
There are 2 independent parts, one for each index of `dp`. The reference program is written for one: setup_inputs(seed, part) draws one part's arguments, and reference() takes and returns one part's arrays. A program takes and returns all parts, laid end to end along the dimension named above; an argument that names none is the same for every part. Nothing has to cross between parts.
Inputs may be any that keep to these rules, and one draw needn't show every extreme that they name: Each row and each column of counts sums to 128; every loader sends 12 rows to exactly one device. For each device d the ranges from offsets[j, d] to offsets[j, d] + counts[j, d] - 1 over all loaders j tile 0 to 127.
All inputs are finite; a program needn't handle non-finite values.
Results may differ from the reference program's by a relative error of at most 0.0023.
Values may be sent and summed in bfloat16 or wider, within the bound.
A program may use at most 192 MiB of HBM per device.

```python
import jax
import jax.numpy as jnp
from jax import lax

HEADS = 16
HEAD = 64
FEAT = 256
VDIM = 64
TOK_DEV = 128
TOKENS = 2048
BASE = 8
SPREAD = 4
N_SEQ = 16


def route_tables(key):
    table_key = jax.random.fold_in(key, 7)
    first_key, second_key, third_key = jax.random.split(table_key, 3)
    sigma = jax.random.permutation(first_key, N_SEQ).astype(jnp.int32)
    shifts = jax.random.randint(second_key, (SPREAD,), 1, N_SEQ).astype(jnp.int32)
    loaders = jnp.arange(N_SEQ, dtype=jnp.int32)
    peak = (loaders[None, :] == sigma[:, None]).astype(jnp.int32)
    taken_index = sigma[(loaders[None, :] + shifts[:, None]) % N_SEQ]
    taken = jnp.sum((taken_index[:, :, None] == loaders[None, None, :]).astype(jnp.int32), axis=0)
    counts = (BASE + SPREAD * peak - taken).astype(jnp.int32)
    order_keys = jax.random.split(third_key, N_SEQ)
    ranks = jax.vmap(lambda one_key: jax.random.permutation(one_key, N_SEQ))(order_keys).T.astype(jnp.int32)
    before = (ranks[None, :, :] < ranks[:, None, :]).astype(jnp.int32)
    offsets = jnp.sum(before * counts[None, :, :], axis=1).astype(jnp.int32)
    return (counts, offsets)


def draw_counts(key, part):
    return route_tables(key)[0]


def draw_offsets(key, part):
    return route_tables(key)[1]


def draw_values(key, part):
    value_key = jax.random.fold_in(key, 11)
    base_key, row_key, column_key = jax.random.split(value_key, 3)
    row_scale = jnp.exp(jax.random.uniform(row_key, (TOKENS, 1), jnp.float32, jnp.log(0.3), jnp.log(3.0)))
    column_scale = jnp.exp(jax.random.uniform(column_key, (1, HEADS * VDIM), jnp.float32, jnp.log(0.3), jnp.log(3.0)))
    basic = jnp.clip(jax.random.normal(base_key, (TOKENS, HEADS * VDIM), jnp.float32), -4.0, 4.0)
    return (basic * row_scale * column_scale).astype(jnp.bfloat16)


def steps_of(key, dims, cuts, least, largest):
    loudness = 1.0
    for dim, shards_of in cuts:
        draws = jax.random.uniform(jax.random.fold_in(jax.random.fold_in(key, 6), dim), (shards_of,), jnp.float32, least / len(cuts), largest / len(cuts))
        loudness = loudness * jnp.repeat(jnp.exp(draws), dims[dim] // shards_of).reshape((-1,) + (1,) * (len(dims) - 1 - dim))
    return loudness


def normal_values(stream_key, dims, spread, most, cuts=(), kind=jnp.bfloat16):
    level = steps_of(stream_key, dims, cuts, -0.22, 0.18) if cuts else 1.0
    entries = jax.random.normal(stream_key, dims, jnp.float32) * spread * level
    return jnp.minimum(jnp.maximum(entries, -most), most).astype(kind)


def setup_inputs(seed: int = 0, part: int = 0) -> dict:
    key_of = jax.random.split(jax.random.key(seed), 8)
    part_keys = jax.random.split(jax.random.fold_in(key_of[7], part), 8)
    queries = normal_values(part_keys[0], (TOKENS, HEADS * HEAD), 1.0, 6.0, ((0, 16),))
    keys = normal_values(part_keys[1], (TOKENS, HEADS * HEAD), 1.0, 6.0, ((0, 16),))
    values = draw_values(jax.random.fold_in(jax.random.fold_in(key_of[7], part), 71), part)
    feat_weight = normal_values(key_of[3], (HEADS, HEAD, FEAT), HEAD ** -0.5, 0.75)
    norm_gain = jnp.clip(1.0 + 0.15 * jax.random.normal(key_of[4], (HEADS * VDIM,), jnp.float32), 0.25, 1.75).astype(jnp.bfloat16)
    counts = draw_counts(jax.random.fold_in(jax.random.fold_in(key_of[7], part), 71), part)
    offsets = draw_offsets(jax.random.fold_in(jax.random.fold_in(key_of[7], part), 71), part)
    return {"queries": queries, "keys": keys, "values": values, "feat_weight": feat_weight, "norm_gain": norm_gain, "counts": counts, "offsets": offsets}


def trace_positions(counts, offsets):
    starts = (jnp.cumsum(counts, axis=1) - counts).astype(jnp.int32)
    inner = jnp.arange(TOK_DEV, dtype=jnp.int32)
    device_ids = jnp.arange(N_SEQ, dtype=jnp.int32)

    def one_loader(start_row, count_row, offset_row):
        inside = (inner[:, None] >= start_row[None, :]) & (inner[:, None] < (start_row + count_row)[None, :])
        hot = inside.astype(jnp.int32)
        target = lax.optimization_barrier(jnp.sum(hot * device_ids[None, :], axis=1)).astype(jnp.int32)
        shift = lax.optimization_barrier(jnp.sum(hot * (offset_row - start_row)[None, :], axis=1)).astype(jnp.int32)
        return (target * TOK_DEV + shift + inner).astype(jnp.int32)
    return jax.vmap(one_loader)(starts, counts, offsets).reshape(-1)

def feature_map(rows, feat_weight):
    split_rows = rows.reshape(rows.shape[0], HEADS, HEAD).astype(jnp.float32)
    projected = jnp.einsum('thd,hdf->htf', split_rows, feat_weight.astype(jnp.float32), precision=lax.Precision.HIGHEST)
    return (jax.nn.elu(projected) + 1.0).astype(jnp.bfloat16)

def reference(queries, keys, values, feat_weight, norm_gain, counts, offsets):
    position = trace_positions(counts, offsets)
    packed_q = jnp.zeros(queries.shape, queries.dtype).at[position].set(queries)
    packed_k = jnp.zeros(keys.shape, keys.dtype).at[position].set(keys)
    packed_v = jnp.zeros(values.shape, values.dtype).at[position].set(values)
    inner = jnp.arange(TOK_DEV, dtype=jnp.int32)
    causal = inner[:, None] >= inner[None, :]
    gain = norm_gain.astype(jnp.float32).reshape(HEADS, 1, VDIM)

    def block_step(state, block):
        block_q, block_k, block_v = block
        phi_query = feature_map(block_q, feat_weight).astype(jnp.float32)
        phi_key = feature_map(block_k, feat_weight).astype(jnp.float32)
        value_heads = block_v.reshape(TOK_DEV, HEADS, VDIM).transpose(1, 0, 2).astype(jnp.float32)
        scores = jnp.einsum('hsf,htf->hst', phi_query, phi_key, precision=lax.Precision.HIGHEST)
        scores = jnp.where(causal[None, :, :], scores, 0.0)
        attended = jnp.einsum('hst,htv->hsv', scores, value_heads, precision=lax.Precision.HIGHEST)
        attended = attended + jnp.einsum('hsf,hfv->hsv', phi_query, state, precision=lax.Precision.HIGHEST)
        state = state + jnp.einsum('htf,htv->hfv', phi_key, value_heads, precision=lax.Precision.HIGHEST)
        centre = lax.optimization_barrier(jnp.mean(attended, axis=2, keepdims=True))
        centred = attended - centre
        spread_sq = lax.optimization_barrier(jnp.mean(centred * centred, axis=2, keepdims=True))
        normed = centred * lax.rsqrt(spread_sq + 1e-05) * gain
        return (state, normed.transpose(1, 0, 2).reshape(TOK_DEV, HEADS * VDIM).astype(jnp.bfloat16))
    blocks = (packed_q.reshape(N_SEQ, TOK_DEV, -1), packed_k.reshape(N_SEQ, TOK_DEV, -1), packed_v.reshape(N_SEQ, TOK_DEV, -1))
    initial = jnp.zeros((HEADS, FEAT, VDIM), jnp.float32)
    final_state, normed_blocks = lax.scan(block_step, initial, blocks)
    normed = normed_blocks.reshape(TOKENS, HEADS * VDIM)
    return normed[position]
```

```python
import functools

import jax
import jax.numpy as jnp
from jax import lax
from jax.experimental import pallas as pl
from jax.experimental.pallas import tpu as pltpu
from jax.sharding import PartitionSpec as P

MESH = pl.DeviceIdType.MESH
F32 = jnp.float32
BF16 = jnp.bfloat16


def kernel(
    n,
    heads,
    q_ref,
    k_ref,
    v_ref,
    w_ref,
    gain_ref,
    counts_ref,
    offsets_ref,
    out_ref,
    send,
    recv,
    phi_q,
    phi_kt,
    val,
    posr,
    post,
    posc,
    wq,
    wkt,
    out_send,
    out_recv,
    send_sem,
    recv_sem,
    back_send_sem,
    back_recv_sem,
):
    rows = q_ref.shape[0]
    half = rows // 2
    width = q_ref.shape[1] // heads
    feat = w_ref.shape[2]
    group = n // heads
    part_rows = rows // group
    part_half = part_rows // 2
    total = n * rows
    queries = n * part_rows
    me = lax.axis_index("seq")
    head = me // group
    part = me % group

    barrier = pltpu.get_barrier_semaphore()

    def greet(step, carry):
        peer = lax.rem(me + step, n)
        pl.semaphore_signal(barrier, inc=1, device_id={"seq": peer}, device_id_type=MESH)
        return carry

    lax.fori_loop(1, n, greet, 0)

    for pair in range(heads // 2):
        lanes = slice(2 * width * pair, 2 * width * (pair + 1))
        q = q_ref[:, lanes]
        k = k_ref[:, lanes]
        v = v_ref[:, lanes]
        send[2 * pair, 0:rows, :] = jnp.concatenate([q[:, :width], k[:, :width]], axis=1)
        send[2 * pair + 1, 0:rows, :] = jnp.concatenate([q[:, width:], k[:, width:]], axis=1)
        send[2 * pair, rows:, :] = jnp.concatenate([v[:half, :width], v[half:, :width]], axis=1)
        send[2 * pair + 1, rows:, :] = jnp.concatenate([v[:half, width:], v[half:, width:]], axis=1)

    pl.semaphore_wait(barrier, n - 1)

    def forward(peer):
        return pltpu.make_async_remote_copy(
            src_ref=send.at[peer // group],
            dst_ref=recv.at[me],
            send_sem=send_sem.at[peer],
            recv_sem=recv_sem.at[me],
            device_id={"seq": peer},
            device_id_type=MESH,
        )

    def send_one(step, carry):
        forward(lax.rem(me + step, n)).start()
        return carry

    lax.fori_loop(1, n, send_one, 0)
    recv[me] = send[head]

    lane = lax.broadcasted_iota(jnp.int32, (n, rows), 1)
    start = jnp.zeros((n, 1), jnp.int32)
    position = lane
    for d in range(n):
        count = counts_ref[:, d : d + 1]
        inside = (lane >= start) & (lane < start + count)
        position = position + jnp.where(inside, d * rows + offsets_ref[:, d : d + 1] - start, 0)
        start = start + count
    position = position.astype(F32)
    posr[...] = position
    if n < rows:
        position = jnp.concatenate([position, jnp.zeros((rows - n, rows), F32)], axis=0)
    post[...] = position.T
    mine = post[pl.ds(pl.multiple_of(part * part_rows, part_rows), part_rows), :]
    for j in range(n):
        posc[j * part_rows : (j + 1) * part_rows, :] = jnp.broadcast_to(
            mine[:, j : j + 1], (part_rows, 128)
        )

    w = w_ref[head]
    blank = jnp.zeros_like(w)
    wq[...] = jnp.concatenate([w, blank], axis=0)
    wkt[...] = jnp.concatenate([blank, w], axis=0).astype(F32).T.astype(BF16)
    gain = jnp.zeros((1, width), F32)
    for h in range(heads):
        gain = gain + jnp.where(head == h, gain_ref[:, h * width : (h + 1) * width].astype(F32), 0.0)

    def feature(z):
        return jnp.where(z > 0.0, z + 1.0, jnp.exp(jnp.minimum(z, 0.0))).astype(BF16)

    def take_block(src):
        x = recv[src, 0:rows, :]
        keys = lax.dot_general(wkt[...], x, (((1,), (1,)), ((), ())), preferred_element_type=F32)
        phi_kt[:, pl.ds(pl.multiple_of(src * rows, rows), rows)] = feature(keys)
        xq = recv[src, pl.ds(pl.multiple_of(part * part_rows, part_rows), part_rows), :]
        proj = jnp.dot(xq, wq[...], preferred_element_type=F32)
        phi_q[pl.ds(pl.multiple_of(src * part_rows, part_rows), part_rows), :] = feature(proj)
        block = recv[src, rows:, :]
        val[pl.ds(pl.multiple_of(src * rows, rows), half), :] = block[:, :width]
        val[pl.ds(pl.multiple_of(src * rows + half, half), half), :] = block[:, width:]

    take_block(me)

    def arrive(step, carry):
        src = lax.rem(me + n - step, n)
        pltpu.make_async_remote_copy(
            src_ref=send.at[0],
            dst_ref=recv.at[src],
            send_sem=send_sem.at[src],
            recv_sem=recv_sem.at[src],
            device_id={"seq": src},
            device_id_type=MESH,
        ).wait_recv()
        take_block(src)
        return carry

    lax.fori_loop(1, n, arrive, 0)

    tile_r = min(512, queries)
    tile_s = min(512, total)
    per_r = tile_r // part_rows
    per_s = tile_s // rows
    blocks = queries // tile_r

    def back(loader):
        return pltpu.make_async_remote_copy(
            src_ref=out_send.at[loader],
            dst_ref=out_recv.at[me],
            send_sem=back_send_sem.at[loader],
            recv_sem=back_recv_sem.at[me],
            device_id={"seq": loader},
            device_id_type=MESH,
        )

    def attend(step, carry):
        rb = lax.rem(me // per_r + step, blocks)
        r0 = pl.multiple_of(rb * tile_r, tile_r)
        fq = phi_q[pl.ds(r0, tile_r), :]
        pc = posc[pl.ds(r0, tile_r), :]
        pc = jnp.concatenate([pc] * per_s, axis=1)

        def over(sb, acc):
            s0 = pl.multiple_of(sb * tile_s, tile_s)
            scores = jnp.dot(fq, phi_kt[:, pl.ds(s0, tile_s)], preferred_element_type=F32)
            pr = jnp.concatenate([posr[pl.ds(sb * per_s + i, 1), :] for i in range(per_s)], axis=1)
            scores = jnp.where(pr <= pc, scores, 0.0)
            high = scores.astype(BF16)
            low = (scores - high.astype(F32)).astype(BF16)
            vals = val[pl.ds(s0, tile_s), :]
            return (
                acc
                + jnp.dot(high, vals, preferred_element_type=F32)
                + jnp.dot(low, vals, preferred_element_type=F32)
            )

        attended = lax.fori_loop(0, total // tile_s, over, jnp.zeros((tile_r, width), F32))
        centre = jnp.mean(attended, axis=1, keepdims=True)
        centred = attended - centre
        spread = jnp.mean(centred * centred, axis=1, keepdims=True)
        normed = (centred * lax.rsqrt(spread + 1e-05) * gain).astype(BF16)
        for i in range(per_r):
            y = normed[i * part_rows : (i + 1) * part_rows]
            loader = rb * per_r + i
            out_send[loader] = jnp.concatenate([y[:part_half], y[part_half:]], axis=1)

        for i in range(per_r):
            loader = rb * per_r + i

            @pl.when(loader != me)
            def _():
                back(loader).start()

        return carry

    lax.fori_loop(0, blocks, attend, 0)
    out_recv[me] = out_send[me]

    def finish(step, carry):
        src = lax.rem(me + n - step, n)
        pltpu.make_async_remote_copy(
            src_ref=out_send.at[src],
            dst_ref=out_recv.at[src],
            send_sem=back_send_sem.at[src],
            recv_sem=back_recv_sem.at[src],
            device_id={"seq": src},
            device_id_type=MESH,
        ).wait_recv()
        return carry

    lax.fori_loop(1, n, finish, 0)

    for piece in range(group):
        first = slice(piece * part_rows, piece * part_rows + part_half)
        second = slice(piece * part_rows + part_half, (piece + 1) * part_rows)
        for pair in range(heads // 2):
            lanes = slice(2 * width * pair, 2 * width * (pair + 1))
            a = out_recv[2 * pair * group + piece]
            b = out_recv[(2 * pair + 1) * group + piece]
            out_ref[first, lanes] = jnp.concatenate([a[:, :width], b[:, :width]], axis=1)
            out_ref[second, lanes] = jnp.concatenate([a[:, width:], b[:, width:]], axis=1)

    def drain(step, carry):
        peer = lax.rem(me + step, n)
        forward(peer).wait_send()
        back(peer).wait_send()
        return carry

    lax.fori_loop(1, n, drain, 0)


def per_device(n, queries, keys, values, feat_weight, norm_gain, counts, offsets):
    rows = queries.shape[0]
    heads, width, feat = feat_weight.shape
    group = n // heads
    part_rows = rows // group
    total = n * rows
    lanes = 2 * width
    return pl.pallas_call(
        functools.partial(kernel, n, heads),
        out_shape=jax.ShapeDtypeStruct(queries.shape, BF16),
        in_specs=[pl.BlockSpec(memory_space=pltpu.VMEM)] * 7,
        out_specs=pl.BlockSpec(memory_space=pltpu.VMEM),
        scratch_shapes=[
            pltpu.VMEM((heads, rows + rows // 2, lanes), BF16),
            pltpu.VMEM((n, rows + rows // 2, lanes), BF16),
            pltpu.VMEM((n * part_rows, feat), BF16),
            pltpu.VMEM((feat, total), BF16),
            pltpu.VMEM((total, width), BF16),
            pltpu.VMEM((n, rows), F32),
            pltpu.VMEM((rows, max(n, rows)), F32),
            pltpu.VMEM((n * part_rows, 128), F32),
            pltpu.VMEM((lanes, feat), BF16),
            pltpu.VMEM((feat, lanes), BF16),
            pltpu.VMEM((n, part_rows // 2, lanes), BF16),
            pltpu.VMEM((n, part_rows // 2, lanes), BF16),
            pltpu.SemaphoreType.DMA((n,)),
            pltpu.SemaphoreType.DMA((n,)),
            pltpu.SemaphoreType.DMA((n,)),
            pltpu.SemaphoreType.DMA((n,)),
        ],
        compiler_params=pltpu.CompilerParams(
            collective_id=0, has_side_effects=True, vmem_limit_bytes=48 * 1024 * 1024
        ),
    )(queries, keys, values, feat_weight, norm_gain.reshape(1, -1), counts, offsets)


def solution(mesh):
    in_specs = (
        P(("dp", "seq"), None),
        P(("dp", "seq"), None),
        P(("dp", "seq"), None),
        P(),
        P(),
        P("dp", None),
        P("dp", None),
    )
    return jax.shard_map(
        functools.partial(per_device, mesh.shape["seq"]),
        mesh=mesh,
        in_specs=in_specs,
        out_specs=P(("dp", "seq"), None),
        check_vma=False,
    )
```

```python
import functools

import jax
import jax.numpy as jnp
from jax import lax
from jax.experimental import pallas as pl
from jax.experimental.pallas import tpu as pltpu
from jax.sharding import PartitionSpec as P

MESH = pl.DeviceIdType.MESH
F32 = jnp.float32
BF16 = jnp.bfloat16
GROUPS = 4


def kernel(
    n,
    heads,
    q_ref,
    k_ref,
    v_ref,
    w_ref,
    gain_ref,
    counts_ref,
    offsets_ref,
    out_ref,
    q_buf,
    k_buf,
    v_buf,
    w_buf,
    gain_buf,
    counts_buf,
    offsets_buf,
    load_sem,
    send,
    recv,
    phi_q,
    phi_kt,
    val,
    posr,
    post,
    posc,
    slot_row,
    slot_col,
    acc,
    wq,
    wkt,
    out_send,
    out_recv,
    send_sem,
    recv_sem,
    back_send_sem,
    back_recv_sem,
):
    rows = q_ref.shape[0]
    half = rows // 2
    width = q_ref.shape[1] // heads
    feat = w_ref.shape[2]
    group = n // heads
    part_rows = rows // group
    part_half = part_rows // 2
    total = n * rows
    queries = n * part_rows
    me = lax.axis_index("seq")
    head = me // group
    part = me % group

    half_ring = n // 2
    own = me // half_ring * half_ring
    other = lax.rem(own + half_ring, n)

    def target(step):
        return jnp.where(step < half_ring, own, other) + lax.rem(me + step, half_ring)

    def source(step):
        return jnp.where(step < half_ring, own, other) + lax.rem(me + n - step, half_ring)

    loads = [
        pltpu.make_async_copy(src, dst, load_sem.at[i])
        for i, (src, dst) in enumerate(
            (
                (q_ref, q_buf),
                (k_ref, k_buf),
                (v_ref, v_buf),
                (counts_ref, counts_buf),
                (offsets_ref, offsets_buf),
                (w_ref.at[head], w_buf),
                (gain_ref, gain_buf),
            )
        )
    ]
    for load in loads:
        load.start()

    barrier = pltpu.get_barrier_semaphore()

    def greet(step, carry):
        peer = lax.rem(me + step, n)
        pl.semaphore_signal(barrier, inc=1, device_id={"seq": peer}, device_id_type=MESH)
        return carry

    lax.fori_loop(1, n, greet, 0)

    for load in loads[:3]:
        load.wait()

    for pair in range(heads // 2):
        lanes = slice(2 * width * pair, 2 * width * (pair + 1))
        q = q_buf[:, lanes]
        k = k_buf[:, lanes]
        v = v_buf[:, lanes]
        send[2 * pair, 0:rows, :] = jnp.concatenate([q[:, :width], k[:, :width]], axis=1)
        send[2 * pair + 1, 0:rows, :] = jnp.concatenate([q[:, width:], k[:, width:]], axis=1)
        send[2 * pair, rows:, :] = jnp.concatenate([v[:half, :width], v[half:, :width]], axis=1)
        send[2 * pair + 1, rows:, :] = jnp.concatenate([v[:half, width:], v[half:, width:]], axis=1)

    pl.semaphore_wait(barrier, n - 1)

    def forward(peer):
        return pltpu.make_async_remote_copy(
            src_ref=send.at[peer // group],
            dst_ref=recv.at[me],
            send_sem=send_sem.at[peer],
            recv_sem=recv_sem.at[me],
            device_id={"seq": peer},
            device_id_type=MESH,
        )

    def send_one(step, carry):
        forward(target(step)).start()
        return carry

    lax.fori_loop(1, n, send_one, 0)
    recv[me] = send[head]

    for load in loads[3:]:
        load.wait()

    lane = lax.broadcasted_iota(jnp.int32, (n, rows), 1)
    start = jnp.zeros((n, 1), jnp.int32)
    position = lane
    for d in range(n):
        count = counts_buf[:, d : d + 1]
        inside = (lane >= start) & (lane < start + count)
        position = position + jnp.where(inside, d * rows + offsets_buf[:, d : d + 1] - start, 0)
        start = start + count
    position = position.astype(F32)
    posr[...] = position
    if n < rows:
        position = jnp.concatenate([position, jnp.zeros((rows - n, rows), F32)], axis=0)
    post[...] = position.T
    mine = post[pl.ds(pl.multiple_of(part * part_rows, part_rows), part_rows), :]
    for j in range(n):
        posc[j * part_rows : (j + 1) * part_rows, :] = jnp.broadcast_to(
            mine[:, j : j + 1], (part_rows, 128)
        )

    w = w_buf[...]
    blank = jnp.zeros_like(w)
    wq[...] = jnp.concatenate([w, blank], axis=0)
    wkt[...] = jnp.concatenate([blank, w], axis=0).astype(F32).T.astype(BF16)
    gain = jnp.zeros((1, width), F32)
    for h in range(heads):
        gain = gain + jnp.where(head == h, gain_buf[:, h * width : (h + 1) * width].astype(F32), 0.0)

    def feature(z):
        return jnp.where(z > 0.0, z + 1.0, jnp.exp(jnp.minimum(z, 0.0))).astype(BF16)

    def take_block(step):
        src = source(step)
        x = recv[src, 0:rows, :]
        keys = lax.dot_general(wkt[...], x, (((1,), (1,)), ((), ())), preferred_element_type=F32)
        phi_kt[:, step * rows : (step + 1) * rows] = feature(keys)
        mine_of = pl.multiple_of(part * part_rows, part_rows)
        proj = jnp.dot(
            recv[src, pl.ds(mine_of, part_rows), :], wq[...], preferred_element_type=F32
        )
        slots = slice(step * part_rows, (step + 1) * part_rows)
        phi_q[slots, :] = feature(proj)
        block = recv[src, rows:, :]
        val[step * rows : step * rows + half, :] = block[:, :width]
        val[step * rows + half : (step + 1) * rows, :] = block[:, width:]
        slot_row[step : step + 1, :] = posr[pl.ds(src, 1), :]
        slot_col[slots, :] = posc[
            pl.ds(pl.multiple_of(src * part_rows, part_rows), part_rows), :
        ]

    def arrive(step):
        src = source(step)
        pltpu.make_async_remote_copy(
            src_ref=send.at[0],
            dst_ref=recv.at[src],
            send_sem=send_sem.at[src],
            recv_sem=recv_sem.at[src],
            device_id={"seq": src},
            device_id_type=MESH,
        ).wait_recv()

    groups = min(GROUPS, n)
    per = n // groups
    tile_r = per * part_rows
    tile_s = per * rows

    def tile(rb, sb):
        r0 = pl.multiple_of(rb * tile_r, tile_r)
        s0 = pl.multiple_of(sb * tile_s, tile_s)
        scores = jnp.dot(
            phi_q[pl.ds(r0, tile_r), :], phi_kt[:, pl.ds(s0, tile_s)], preferred_element_type=F32
        )
        later = jnp.concatenate([slot_col[pl.ds(r0, tile_r), :]] * per, axis=1)
        earlier = jnp.concatenate([slot_row[pl.ds(sb * per + i, 1), :] for i in range(per)], axis=1)
        scores = jnp.where(earlier <= later, scores, 0.0)
        high = scores.astype(BF16)
        low = (scores - high.astype(F32)).astype(BF16)
        vals = val[pl.ds(s0, tile_s), :]
        return jnp.dot(high, vals, preferred_element_type=F32) + jnp.dot(
            low, vals, preferred_element_type=F32
        )

    def back(step):
        loader = source(step)
        return pltpu.make_async_remote_copy(
            src_ref=out_send.at[step],
            dst_ref=out_recv.at[me],
            send_sem=back_send_sem.at[loader],
            recv_sem=back_recv_sem.at[me],
            device_id={"seq": loader},
            device_id_type=MESH,
        )

    def finish(rb, attended):
        centre = jnp.mean(attended, axis=1, keepdims=True)
        centred = attended - centre
        spread = jnp.mean(centred * centred, axis=1, keepdims=True)
        normed = (centred * lax.rsqrt(spread + 1e-05) * gain).astype(BF16)
        for i in range(per):
            y = normed[i * part_rows : (i + 1) * part_rows]
            out_send[rb * per + i] = jnp.concatenate([y[:part_half], y[part_half:]], axis=1)
        for i in range(per):
            if rb * per + i > 0:
                back(rb * per + i).start()

    def rows_of(rb):
        return pl.ds(pl.multiple_of(rb * tile_r, tile_r), tile_r)

    for gi in range(groups):
        for step in range(gi * per, (gi + 1) * per):
            if step > 0:
                arrive(step)
            take_block(step)
        last = gi == groups - 1
        fresh = tile(gi, gi)
        if not last:

            def both(i, fresh):
                acc[rows_of(i), :] = acc[rows_of(i), :] + tile(i, gi)
                return fresh + tile(gi, i)

            acc[rows_of(gi), :] = lax.fori_loop(0, gi, both, fresh)
        else:
            finish(gi, lax.fori_loop(0, gi, lambda i, fresh: fresh + tile(gi, i), fresh))
            for i in reversed(range(gi)):
                finish(i, acc[rows_of(i), :] + tile(i, gi))
    out_recv[me] = out_send[0]

    def collect(step, carry):
        src = source(step)
        pltpu.make_async_remote_copy(
            src_ref=out_send.at[step],
            dst_ref=out_recv.at[src],
            send_sem=back_send_sem.at[src],
            recv_sem=back_recv_sem.at[src],
            device_id={"seq": src},
            device_id_type=MESH,
        ).wait_recv()
        return carry

    lax.fori_loop(1, n, collect, 0)

    for piece in range(group):
        first = slice(piece * part_rows, piece * part_rows + part_half)
        second = slice(piece * part_rows + part_half, (piece + 1) * part_rows)
        for pair in range(heads // 2):
            lanes = slice(2 * width * pair, 2 * width * (pair + 1))
            a = out_recv[2 * pair * group + piece]
            b = out_recv[(2 * pair + 1) * group + piece]
            out_ref[first, lanes] = jnp.concatenate([a[:, :width], b[:, :width]], axis=1)
            out_ref[second, lanes] = jnp.concatenate([a[:, width:], b[:, width:]], axis=1)

    def drain(step, carry):
        peer = target(step)
        forward(peer).wait_send()
        back(step).wait_send()
        return carry

    lax.fori_loop(1, n, drain, 0)


def per_device(n, queries, keys, values, feat_weight, norm_gain, counts, offsets):
    rows = queries.shape[0]
    heads, width, feat = feat_weight.shape
    group = n // heads
    part_rows = rows // group
    total = n * rows
    lanes = 2 * width
    return pl.pallas_call(
        functools.partial(kernel, n, heads),
        out_shape=jax.ShapeDtypeStruct(queries.shape, BF16),
        in_specs=[pl.BlockSpec(memory_space=pltpu.HBM)] * 7,
        out_specs=pl.BlockSpec(memory_space=pltpu.VMEM),
        scratch_shapes=[
            pltpu.VMEM(queries.shape, BF16),
            pltpu.VMEM(keys.shape, BF16),
            pltpu.VMEM(values.shape, BF16),
            pltpu.VMEM((width, feat), BF16),
            pltpu.VMEM((1, norm_gain.shape[0]), BF16),
            pltpu.VMEM(counts.shape, jnp.int32),
            pltpu.VMEM(offsets.shape, jnp.int32),
            pltpu.SemaphoreType.DMA((7,)),
            pltpu.VMEM((heads, rows + rows // 2, lanes), BF16),
            pltpu.VMEM((n, rows + rows // 2, lanes), BF16),
            pltpu.VMEM((n * part_rows, feat), BF16),
            pltpu.VMEM((feat, total), BF16),
            pltpu.VMEM((total, width), BF16),
            pltpu.VMEM((n, rows), F32),
            pltpu.VMEM((rows, max(n, rows)), F32),
            pltpu.VMEM((n * part_rows, 128), F32),
            pltpu.VMEM((n, rows), F32),
            pltpu.VMEM((n * part_rows, 128), F32),
            pltpu.VMEM((n * part_rows, width), F32),
            pltpu.VMEM((lanes, feat), BF16),
            pltpu.VMEM((feat, lanes), BF16),
            pltpu.VMEM((n, part_rows // 2, lanes), BF16),
            pltpu.VMEM((n, part_rows // 2, lanes), BF16),
            pltpu.SemaphoreType.DMA((n,)),
            pltpu.SemaphoreType.DMA((n,)),
            pltpu.SemaphoreType.DMA((n,)),
            pltpu.SemaphoreType.DMA((n,)),
        ],
        compiler_params=pltpu.CompilerParams(
            collective_id=0, has_side_effects=True, vmem_limit_bytes=48 * 1024 * 1024
        ),
    )(queries, keys, values, feat_weight, norm_gain.reshape(1, -1), counts, offsets)


def solution(mesh):
    in_specs = (
        P(("dp", "seq"), None),
        P(("dp", "seq"), None),
        P(("dp", "seq"), None),
        P(),
        P(),
        P("dp", None),
        P("dp", None),
    )
    return jax.shard_map(
        functools.partial(per_device, mesh.shape["seq"]),
        mesh=mesh,
        in_specs=in_specs,
        out_specs=P(("dp", "seq"), None),
        check_vma=False,
    )
```

```python
import functools

import jax
import jax.numpy as jnp
from jax import lax
from jax.experimental import pallas as pl
from jax.experimental.pallas import tpu as pltpu
from jax.sharding import PartitionSpec as P

MESH = pl.DeviceIdType.MESH
F32 = jnp.float32
BF16 = jnp.bfloat16
GROUPS = 4


def kernel(
    n,
    heads,
    q_ref,
    k_ref,
    v_ref,
    w_ref,
    gain_ref,
    counts_ref,
    offsets_ref,
    out_ref,
    q_buf,
    k_buf,
    v_buf,
    w_buf,
    gain_buf,
    counts_buf,
    offsets_buf,
    load_sem,
    send,
    recv,
    phi_q,
    phi_kt,
    val,
    posr,
    post,
    posc,
    slot_row,
    slot_col,
    acc,
    wq,
    wkt,
    out_send,
    out_recv,
    send_sem,
    recv_sem,
    back_send_sem,
    back_recv_sem,
):
    rows = q_ref.shape[0]
    half = rows // 2
    width = q_ref.shape[1] // heads
    feat = w_ref.shape[2]
    group = n // heads
    part_rows = rows // group
    part_half = part_rows // 2
    total = n * rows
    queries = n * part_rows
    me = lax.axis_index("seq")
    head = me // group
    part = me % group

    half_ring = n // 2
    own = me // half_ring * half_ring
    other = lax.rem(own + half_ring, n)

    def target(step):
        return jnp.where(step < half_ring, own, other) + lax.rem(me + step, half_ring)

    def source(step):
        return jnp.where(step < half_ring, own, other) + lax.rem(me + n - step, half_ring)

    loads = [
        pltpu.make_async_copy(src, dst, load_sem.at[i])
        for i, (src, dst) in enumerate(
            (
                (q_ref, q_buf),
                (k_ref, k_buf),
                (v_ref, v_buf),
                (counts_ref, counts_buf),
                (offsets_ref, offsets_buf),
                (w_ref.at[head], w_buf),
                (gain_ref, gain_buf),
            )
        )
    ]
    for load in loads:
        load.start()

    barrier = pltpu.get_barrier_semaphore()

    def greet(step, carry):
        peer = lax.rem(me + step, n)
        pl.semaphore_signal(barrier, inc=1, device_id={"seq": peer}, device_id_type=MESH)
        return carry

    lax.fori_loop(1, n, greet, 0)

    for load in loads[:3]:
        load.wait()

    for pair in range(heads // 2):
        lanes = slice(2 * width * pair, 2 * width * (pair + 1))
        q = q_buf[:, lanes]
        k = k_buf[:, lanes]
        v = v_buf[:, lanes]
        send[2 * pair, 0:rows, :] = jnp.concatenate([q[:, :width], k[:, :width]], axis=1)
        send[2 * pair + 1, 0:rows, :] = jnp.concatenate([q[:, width:], k[:, width:]], axis=1)
        send[2 * pair, rows:, :] = jnp.concatenate([v[:half, :width], v[half:, :width]], axis=1)
        send[2 * pair + 1, rows:, :] = jnp.concatenate([v[:half, width:], v[half:, width:]], axis=1)

    pl.semaphore_wait(barrier, n - 1)

    def forward(peer):
        return pltpu.make_async_remote_copy(
            src_ref=send.at[peer // group],
            dst_ref=recv.at[me],
            send_sem=send_sem.at[peer],
            recv_sem=recv_sem.at[me],
            device_id={"seq": peer},
            device_id_type=MESH,
        )

    def send_one(step, carry):
        forward(target(step)).start()
        return carry

    lax.fori_loop(1, n, send_one, 0)
    recv[me] = send[head]

    for load in loads[3:]:
        load.wait()

    lane = lax.broadcasted_iota(jnp.int32, (n, rows), 1)
    start = jnp.zeros((n, 1), jnp.int32)
    position = lane
    for d in range(n):
        count = counts_buf[:, d : d + 1]
        inside = (lane >= start) & (lane < start + count)
        position = position + jnp.where(inside, d * rows + offsets_buf[:, d : d + 1] - start, 0)
        start = start + count
    position = position.astype(F32)
    posr[...] = position
    if n < rows:
        position = jnp.concatenate([position, jnp.zeros((rows - n, rows), F32)], axis=0)
    post[...] = position.T
    mine = post[pl.ds(pl.multiple_of(part * part_rows, part_rows), part_rows), :]
    for j in range(n):
        posc[j * part_rows : (j + 1) * part_rows, :] = jnp.broadcast_to(
            mine[:, j : j + 1], (part_rows, 128)
        )

    w = w_buf[...]
    blank = jnp.zeros_like(w)
    wq[...] = jnp.concatenate([w, blank], axis=0)
    wkt[...] = jnp.concatenate([blank, w], axis=0).astype(F32).T.astype(BF16)
    gain = jnp.zeros((1, width), F32)
    for h in range(heads):
        gain = gain + jnp.where(head == h, gain_buf[:, h * width : (h + 1) * width].astype(F32), 0.0)

    def feature(z):
        return jnp.where(z > 0.0, z + 1.0, jnp.exp(jnp.minimum(z, 0.0))).astype(BF16)

    def take_block(step):
        src = source(step)
        x = recv[src, 0:rows, :]
        keys = lax.dot_general(wkt[...], x, (((1,), (1,)), ((), ())), preferred_element_type=F32)
        phi_kt[:, step * rows : (step + 1) * rows] = feature(keys)
        mine_of = pl.multiple_of(part * part_rows, part_rows)
        proj = jnp.dot(
            recv[src, pl.ds(mine_of, part_rows), :], wq[...], preferred_element_type=F32
        )
        slots = slice(step * part_rows, (step + 1) * part_rows)
        phi_q[slots, :] = feature(proj)
        block = recv[src, rows:, :]
        val[step * rows : step * rows + half, :] = block[:, :width]
        val[step * rows + half : (step + 1) * rows, :] = block[:, width:]
        slot_row[step : step + 1, :] = posr[pl.ds(src, 1), :]
        slot_col[slots, :] = posc[
            pl.ds(pl.multiple_of(src * part_rows, part_rows), part_rows), :
        ]

    def arrive(step):
        src = source(step)
        pltpu.make_async_remote_copy(
            src_ref=send.at[0],
            dst_ref=recv.at[src],
            send_sem=send_sem.at[src],
            recv_sem=recv_sem.at[src],
            device_id={"seq": src},
            device_id_type=MESH,
        ).wait_recv()

    groups = min(GROUPS, n)
    per = n // groups
    tile_r = per * part_rows
    tile_s = per * rows

    def tile(rb, sb):
        r0 = pl.multiple_of(rb * tile_r, tile_r)
        s0 = pl.multiple_of(sb * tile_s, tile_s)
        scores = jnp.dot(
            phi_q[pl.ds(r0, tile_r), :], phi_kt[:, pl.ds(s0, tile_s)], preferred_element_type=F32
        )
        later = jnp.concatenate([slot_col[pl.ds(r0, tile_r), :]] * per, axis=1)
        earlier = jnp.concatenate([slot_row[pl.ds(sb * per + i, 1), :] for i in range(per)], axis=1)
        scores = jnp.where(earlier <= later, scores, 0.0)
        high = scores.astype(BF16)
        low = (scores - high.astype(F32)).astype(BF16)
        vals = val[pl.ds(s0, tile_s), :]
        return jnp.dot(high, vals, preferred_element_type=F32) + jnp.dot(
            low, vals, preferred_element_type=F32
        )

    def back(step):
        loader = source(step)
        return pltpu.make_async_remote_copy(
            src_ref=out_send.at[step],
            dst_ref=out_recv.at[me],
            send_sem=back_send_sem.at[loader],
            recv_sem=back_recv_sem.at[me],
            device_id={"seq": loader},
            device_id_type=MESH,
        )

    def finish(rb, attended):
        centre = jnp.mean(attended, axis=1, keepdims=True)
        centred = attended - centre
        spread = jnp.mean(centred * centred, axis=1, keepdims=True)
        normed = (centred * lax.rsqrt(spread + 1e-05) * gain).astype(BF16)
        for i in range(per):
            y = normed[i * part_rows : (i + 1) * part_rows]
            out_send[rb * per + i] = jnp.concatenate([y[:part_half], y[part_half:]], axis=1)
        for i in range(per):
            if rb * per + i > 0:
                back(rb * per + i).start()

    def rows_of(rb):
        return pl.ds(pl.multiple_of(rb * tile_r, tile_r), tile_r)

    for gi in range(groups):
        for step in range(gi * per, (gi + 1) * per):
            if step > 0:
                arrive(step)
            take_block(step)
        last = gi == groups - 1
        fresh = tile(gi, gi)
        if not last:

            def both(i, fresh):
                acc[rows_of(i), :] = acc[rows_of(i), :] + tile(i, gi)
                return fresh + tile(gi, i)

            acc[rows_of(gi), :] = lax.fori_loop(0, gi, both, fresh)
        else:
            finish(gi, lax.fori_loop(0, gi, lambda i, fresh: fresh + tile(gi, i), fresh))
            for i in reversed(range(gi)):
                finish(i, acc[rows_of(i), :] + tile(i, gi))
    out_recv[me] = out_send[0]

    def collect(step, carry):
        src = source(step)
        pltpu.make_async_remote_copy(
            src_ref=out_send.at[step],
            dst_ref=out_recv.at[src],
            send_sem=back_send_sem.at[src],
            recv_sem=back_recv_sem.at[src],
            device_id={"seq": src},
            device_id_type=MESH,
        ).wait_recv()
        return carry

    lax.fori_loop(1, n, collect, 0)

    for piece in range(group):
        first = slice(piece * part_rows, piece * part_rows + part_half)
        second = slice(piece * part_rows + part_half, (piece + 1) * part_rows)
        for pair in range(heads // 2):
            lanes = slice(2 * width * pair, 2 * width * (pair + 1))
            a = out_recv[2 * pair * group + piece]
            b = out_recv[(2 * pair + 1) * group + piece]
            out_ref[first, lanes] = jnp.concatenate([a[:, :width], b[:, :width]], axis=1)
            out_ref[second, lanes] = jnp.concatenate([a[:, width:], b[:, width:]], axis=1)

    def drain(step, carry):
        peer = target(step)
        forward(peer).wait_send()
        back(step).wait_send()
        return carry

    lax.fori_loop(1, n, drain, 0)


def per_device(n, queries, keys, values, feat_weight, norm_gain, counts, offsets):
    rows = queries.shape[0]
    heads, width, feat = feat_weight.shape
    group = n // heads
    part_rows = rows // group
    total = n * rows
    lanes = 2 * width
    return pl.pallas_call(
        functools.partial(kernel, n, heads),
        out_shape=jax.ShapeDtypeStruct(queries.shape, BF16),
        in_specs=[pl.BlockSpec(memory_space=pltpu.HBM)] * 7,
        out_specs=pl.BlockSpec(memory_space=pltpu.VMEM),
        scratch_shapes=[
            pltpu.VMEM(queries.shape, BF16),
            pltpu.VMEM(keys.shape, BF16),
            pltpu.VMEM(values.shape, BF16),
            pltpu.VMEM((width, feat), BF16),
            pltpu.VMEM((1, norm_gain.shape[0]), BF16),
            pltpu.VMEM(counts.shape, jnp.int32),
            pltpu.VMEM(offsets.shape, jnp.int32),
            pltpu.SemaphoreType.DMA((7,)),
            pltpu.VMEM((heads, rows + rows // 2, lanes), BF16),
            pltpu.VMEM((n, rows + rows // 2, lanes), BF16),
            pltpu.VMEM((n * part_rows, feat), BF16),
            pltpu.VMEM((feat, total), BF16),
            pltpu.VMEM((total, width), BF16),
            pltpu.VMEM((n, rows), F32),
            pltpu.VMEM((rows, max(n, rows)), F32),
            pltpu.VMEM((n * part_rows, 128), F32),
            pltpu.VMEM((n, rows), F32),
            pltpu.VMEM((n * part_rows, 128), F32),
            pltpu.VMEM((n * part_rows, width), F32),
            pltpu.VMEM((lanes, feat), BF16),
            pltpu.VMEM((feat, lanes), BF16),
            pltpu.VMEM((n, part_rows // 2, lanes), BF16),
            pltpu.VMEM((n, part_rows // 2, lanes), BF16),
            pltpu.SemaphoreType.DMA((n,)),
            pltpu.SemaphoreType.DMA((n,)),
            pltpu.SemaphoreType.DMA((n,)),
            pltpu.SemaphoreType.DMA((n,)),
        ],
        compiler_params=pltpu.CompilerParams(
            collective_id=0, has_side_effects=True, vmem_limit_bytes=67043328
        ),
    )(queries, keys, values, feat_weight, norm_gain.reshape(1, -1), counts, offsets)


def solution(mesh):
    in_specs = (
        P(("dp", "seq"), None),
        P(("dp", "seq"), None),
        P(("dp", "seq"), None),
        P(),
        P(),
        P("dp", None),
        P("dp", None),
    )
    return jax.shard_map(
        functools.partial(per_device, mesh.shape["seq"]),
        mesh=mesh,
        in_specs=in_specs,
        out_specs=P(("dp", "seq"), None),
        check_vma=False,
    )
```
